32 devices in a mesh: replica: 2 (over core), shard: 16 (over z, y, x).
Axes of the slice: x: 2, y: 2, z: 4, core: 2. Of those that a mesh axis runs over, the one named last changes fastest.
Arguments:
- inner_params: bfloat16 [2, 15360, 4096], P('replica', 'shard'), may hold values from -6 to 6
- anchor: float32 [15360, 4096], P('shard'), may hold values from -6 to 6
- momentum: float32 [15360, 4096], P('shard'), may hold values from -2 to 2
- first_moment: bfloat16 [2, 15360, 4096], P('replica', 'shard'), may hold values from -0.59765625 to 0.59765625
- second_moment: bfloat16 [2, 15360, 4096], P('replica', 'shard'), may hold values from 0.0009994507 to 0.099609375
- activations: bfloat16 [2, 64, 4096], P('replica', 'shard'), may hold values from -6 to 6
- cotangent: bfloat16 [2, 15360, 64], P('replica', 'shard'), may hold values from -6 to 6
- spare_index: int32 [16], P('shard'), may hold values from 0 to 1
- peer_index: int32 [16], P('shard'), may hold values from 0 to 1
Outputs:
- anchor_new: float32 [15360, 4096], P('shard')
- momentum_new: float32 [15360, 4096], P('shard')
- update: float32 [2, 15360, 4096], P('replica', 'shard')
The draws below stay inside these ranges and needn't reach their ends.
Inputs may be any that keep to these rules, and one draw needn't show every extreme that they name: `spare_index`: a replica index for each block. `peer_index`: a replica index for each block; where it equals spare_index the spare keeps its own moments.
All inputs are finite; a program needn't handle non-finite values.
Results may differ from the reference program's by a relative error of at most 0.0018.
Values may be sent and summed in bfloat16 or wider, within the bound.
No kernel may reach another device: no remote copies, remote signals or barrier semaphores. Data moves between devices by JAX's collectives and lax.ppermute only.
A program may use at most 192 MiB of HBM per device.

```python
import math
import jax
import jax.numpy as jnp
from jax import lax

D = 4096
FF = 15360
TOKENS = 64
N_REPLICA = 2
N_SHARD = 16


def with_ends(array, key, least, high):
    longest = array.shape.index(max(array.shape))
    spots = []
    for shift in (0, 1):
        where = [jax.random.randint(jax.random.fold_in(key, axis), (), 0, length) for axis, length in enumerate(array.shape)]
        where[longest] = (where[longest] + shift) % array.shape[longest]
        spots.append(tuple(where))
    return array.at[spots[0]].set(least).at[spots[1]].set(high)


def steps_of(stream_key, dims, shards, low, largest):
    level = 1.0
    for axis_at, parts in shards:
        steps = jax.random.uniform(jax.random.fold_in(jax.random.fold_in(stream_key, 6), axis_at), (parts,), jnp.float32, low / len(shards), largest / len(shards))
        level = level * jnp.repeat(jnp.exp(steps), dims[axis_at] // parts).reshape((-1,) + (1,) * (len(dims) - 1 - axis_at))
    return level


def noise(own_key, dims, deviation, limit, pieces=(), kind=jnp.bfloat16):
    loudness = steps_of(own_key, dims, pieces, -0.22, 0.18) if pieces else 1.0
    values = jax.random.normal(own_key, dims, jnp.float32) * deviation * loudness
    return jnp.minimum(jnp.maximum(values, -limit), limit).astype(kind)


def setup_inputs(seed: int = 0) -> dict:
    key_of = jax.random.split(jax.random.key(seed), 10)
    return {
        "inner_params": noise(key_of[0], (N_REPLICA, FF, D), 1.0, 6.0, ((0, 2), (1, 16))),
        "anchor": noise(key_of[1], (FF, D), 1.0, 6.0, ((0, 16),), jnp.float32),
        "momentum": noise(key_of[2], (FF, D), 0.3, 2.0, ((0, 16),), jnp.float32),
        "first_moment": noise(key_of[3], (N_REPLICA, FF, D), 0.1, 0.59765625, ((0, 2), (1, 16))),
        "second_moment": jnp.clip(jnp.exp(math.log(0.099609375) - 4.6018058 * jax.random.uniform(key_of[4], (N_REPLICA, FF, D), jnp.float32) ** steps_of(key_of[4], (N_REPLICA, FF, D), ((0, 2), (1, 16)), -0.2, 0.2)), 0.0009994507, 0.099609375).astype(jnp.bfloat16),
        "activations": noise(key_of[5], (N_REPLICA, TOKENS, D), 1.0, 6.0, ((0, 2), (1, 16))),
        "cotangent": noise(key_of[6], (N_REPLICA, FF, TOKENS), 1.0, 6.0, ((0, 2), (1, 16))),
        "spare_index": with_ends(jax.random.randint(key_of[7], (N_SHARD,), 0, N_REPLICA), jax.random.fold_in(key_of[7], 1), 0, N_REPLICA - 1).astype(jnp.int32),
        "peer_index": with_ends(jax.random.randint(key_of[8], (N_SHARD,), 0, N_REPLICA), jax.random.fold_in(key_of[8], 1), 0, N_REPLICA - 1).astype(jnp.int32),
    }


outer_rate = 0.7
nesterov_mu = 0.9
beta_one = 0.9
beta_two = 0.95
bias_one = 1.0 - 0.9 ** 40
bias_two = 1.0 - 0.95 ** 40
adam_eps = 1e-08
decay_rate = 0.1

def slope(pre):
    sigma = jax.nn.sigmoid(pre)
    return sigma * (1.0 + pre * (1.0 - sigma))

def reference(inner_params, anchor, momentum, first_moment, second_moment, activations, cotangent, spare_index, peer_index):
    block_rows = FF // N_SHARD
    spare_rows = jnp.repeat(spare_index, block_rows)[:, None]
    peer_rows = jnp.repeat(peer_index, block_rows)[:, None]
    summed = jnp.zeros(anchor.shape, jnp.float32)
    for replica in range(N_REPLICA):
        healthy = (spare_rows != replica).astype(jnp.float32)
        summed = summed + (anchor - inner_params[replica].astype(jnp.float32)) * healthy
    average = summed / (N_REPLICA - 1)
    momentum_new = nesterov_mu * momentum + average
    anchor_new = anchor - outer_rate * (average + nesterov_mu * momentum_new)
    weights = anchor_new.astype(jnp.bfloat16)
    root = math.sqrt(D)

    def replica_update(replica):
        source = jnp.where(replica == spare_rows, peer_rows, replica).astype(jnp.int32)
        first_used = jnp.zeros(anchor.shape, jnp.float32)
        second_used = jnp.zeros(anchor.shape, jnp.float32)
        for other in range(N_REPLICA):
            picked = source == other
            first_used = jnp.where(picked, first_moment[other].astype(jnp.float32), first_used)
            second_used = jnp.where(picked, second_moment[other].astype(jnp.float32), second_used)
        tokens_here = lax.dynamic_index_in_dim(activations, replica, 0, keepdims=False)
        cot_here = lax.dynamic_index_in_dim(cotangent, replica, 0, keepdims=False)
        pre = lax.dot_general(weights, tokens_here, (((1,), (1,)), ((), ())), preferred_element_type=jnp.float32) / root
        grad_pre = (cot_here.astype(jnp.float32) * slope(pre)).astype(jnp.bfloat16)
        gradient = jnp.dot(grad_pre, tokens_here, preferred_element_type=jnp.float32) / root
        first = beta_one * first_used + (1.0 - beta_one) * gradient
        second = beta_two * second_used + (1.0 - beta_two) * gradient * gradient
        return first / bias_one / (jnp.sqrt(second / bias_two) + adam_eps) + decay_rate * anchor_new
    update = lax.map(replica_update, jnp.arange(N_REPLICA, dtype=jnp.int32))
    return (anchor_new, momentum_new, update)
```

```python
import functools
import math

import jax
import jax.numpy as jnp
from jax import lax
from jax.experimental import pallas as pl
from jax.experimental.pallas import tpu as pltpu
from jax.sharding import PartitionSpec as P


outer_rate = 0.7
nesterov_mu = 0.9
beta_one = 0.9
beta_two = 0.95
bias_one = 1.0 - 0.9**40
bias_two = 1.0 - 0.95**40
adam_eps = 1e-08
decay_rate = 0.1

UNIT = 16
LANES = 128
PARTS = ((4,), (6, 3, 2))
OUTER_TILE = 64
ADAM_TILE = 128
DEPTH = 3
OUTER_VMEM = 14
ADAM_VMEM = 26


IN_VMEM = pl.BlockSpec(memory_space=pltpu.VMEM)
IN_HBM = pl.BlockSpec(memory_space=pl.ANY)
IN_SMEM = pl.BlockSpec(memory_space=pltpu.SMEM)


def in_hbm(arrays):
    return [pltpu.with_memory_space_constraint(array, pltpu.HBM) for array in arrays]


def in_vmem(arrays):
    return [pltpu.with_memory_space_constraint(array, pltpu.VMEM) for array in arrays]


def slope(pre):
    sigma = jax.nn.sigmoid(pre)
    return sigma * (1.0 + pre * (1.0 - sigma))


def spans(rows, parts):
    units, total, run, bounds = rows // UNIT, sum(parts), 0, [0]
    for part in parts:
        run += part
        bounds.append(units * run // total * UNIT)
    bounds[-1] = rows
    return [(low, high - low) for low, high in zip(bounds, bounds[1:]) if high > low]


def tile_of(count, limit):
    return max(tile for tile in range(UNIT, max(limit, UNIT) + 1, UNIT) if count % tile == 0)


def stream(steps, loads, stores, compute):
    def load(step):
        for source, ring, sems in loads:
            slot = lax.rem(step, ring.shape[0])
            pltpu.make_async_copy(source(step), ring.at[slot], sems.at[slot]).start()

    def wait_load(step):
        for source, ring, sems in loads:
            slot = lax.rem(step, ring.shape[0])
            pltpu.make_async_copy(source(step), ring.at[slot], sems.at[slot]).wait()

    def wait_store(step):
        for source, target, sems in stores:
            pltpu.make_async_copy(source(step), target(step), sems.at[lax.rem(step, DEPTH)]).wait()

    for step in range(min(DEPTH - 1, steps)):
        load(step)

    def body(step, carry):
        @pl.when(step + DEPTH - 1 < steps)
        def _():
            load(step + DEPTH - 1)

        wait_load(step)

        @pl.when(step >= DEPTH)
        def _():
            wait_store(step - DEPTH)

        compute(step, lax.rem(step, DEPTH))
        for source, target, sems in stores:
            pltpu.make_async_copy(source(step), target(step), sems.at[lax.rem(step, DEPTH)]).start()
        return carry

    lax.fori_loop(0, steps, body, 0)
    for step in range(max(0, steps - DEPTH), steps):
        wait_store(step)


def fetch_kernel(starts, source, *rest):
    targets, sem = rest[:-1], rest[-1]
    copies = [
        pltpu.make_async_copy(source.at[pl.ds(start, target.shape[0])], target, sem.at[at])
        for at, (start, target) in enumerate(zip(starts, targets))
    ]
    for copy in copies:
        copy.start()
    for copy in copies:
        copy.wait()


def fetch(array, chunks):
    width = array.shape[1]
    return pl.pallas_call(
        functools.partial(fetch_kernel, [start for start, _ in chunks]),
        in_specs=[IN_HBM],
        out_specs=[IN_VMEM] * len(chunks),
        out_shape=[pltpu.VMEM((count, width), array.dtype) for _, count in chunks],
        scratch_shapes=[pltpu.SemaphoreType.DMA((len(chunks),))],
        compiler_params=pltpu.CompilerParams(vmem_limit_bytes=OUTER_VMEM * 2**20),
        cost_estimate=pl.CostEstimate(flops=0, bytes_accessed=2 * sum(count for _, count in chunks) * width, transcendentals=0),
        name="fetch",
    )(*in_hbm([array]))


def outer_kernel(start, tile, flags, own, got, anchor, momentum, *rest):
    anchor_out, momentum_out, held, anchor_ring, momentum_ring, moved_ring, sems = rest[-7:]
    spare = flags[0] == 1
    rows = lambda step: pl.ds(pl.multiple_of(start + step * tile, UNIT), tile)

    def compute(step, slot):
        def with_inner(inner):
            base = anchor_ring[slot]
            average = base - inner[pl.ds(pl.multiple_of(step * tile, UNIT), tile), :].astype(jnp.float32)
            moved = nesterov_mu * momentum_ring[slot] + average
            moved_ring[slot] = moved
            held[pl.ds(pl.multiple_of(step * tile, UNIT), tile), :] = base - outer_rate * (average + nesterov_mu * moved)

        @pl.when(spare)
        def _():
            with_inner(got)

        @pl.when(jnp.logical_not(spare))
        def _():
            with_inner(own)

    stream(
        own.shape[0] // tile,
        [
            (lambda step: anchor.at[rows(step)], anchor_ring, sems.at[0]),
            (lambda step: momentum.at[rows(step)], momentum_ring, sems.at[1]),
        ],
        [
            (lambda step: held.at[pl.ds(pl.multiple_of(step * tile, UNIT), tile)], lambda step: anchor_out.at[rows(step)], sems.at[2]),
            (lambda step: moved_ring.at[lax.rem(step, DEPTH)], lambda step: momentum_out.at[rows(step)], sems.at[3]),
        ],
        compute,
    )


def outer_chunk(flags, own, got, anchor, momentum, start, before):
    count, width = own.shape
    tile = tile_of(count, OUTER_TILE)
    whole = pltpu.HBM(anchor.shape, jnp.float32)
    before = list(before or [])
    ring = pltpu.VMEM((DEPTH, tile, width), jnp.float32)
    return pl.pallas_call(
        functools.partial(outer_kernel, start, tile),
        in_specs=[IN_SMEM, IN_VMEM, IN_VMEM, IN_HBM, IN_HBM] + [IN_HBM, IN_HBM][: len(before)],
        out_specs=[IN_HBM, IN_HBM, IN_VMEM],
        out_shape=[whole, whole, pltpu.VMEM((count, width), jnp.float32)],
        input_output_aliases={5: 0, 6: 1} if before else {},
        scratch_shapes=[ring, ring, ring, pltpu.SemaphoreType.DMA((4, DEPTH))],
        compiler_params=pltpu.CompilerParams(vmem_limit_bytes=OUTER_VMEM * 2**20),
        cost_estimate=pl.CostEstimate(flops=10 * count * width, bytes_accessed=16 * count * width, transcendentals=0),
        name="outer",
    )(flags, *in_vmem([own, got]), *in_hbm([anchor, momentum, *before]))


def direction(first, second, raw, root):
    scale = math.sqrt((1.0 - beta_two) / bias_two) / root
    scaled = raw * scale
    mean = first * (beta_one / bias_one) + scaled * ((1.0 - beta_one) / bias_one / root / scale)
    square = second * (beta_two / bias_two) + scaled * scaled
    return mean * pltpu.reciprocal(square * lax.rsqrt(square) + adam_eps, approx=False)


def adam_kernel(start, base, tile, root, pieces, flags, held, cot, first, second, got_first, got_second, *rest):
    parts = rest[:pieces]
    update_out, first_ring, second_ring, update_ring, tokens, sems = rest[-6:]
    rows = lambda at, step: pl.ds(pl.multiple_of(at + step * tile, UNIT), tile)
    height = parts[0].shape[0]
    for index, part in enumerate(parts):
        tokens[index * height : (index + 1) * height, :] = part[...]

    def compute(step, slot):
        weights = held[rows(start - base, step), :]
        pre = lax.dot_general(weights.astype(jnp.bfloat16), tokens[...], (((1,), (1,)), ((), ())), preferred_element_type=jnp.float32) * (1.0 / root)
        grad_pre = (cot[rows(start, step), : tokens.shape[0]].astype(jnp.float32) * slope(pre)).astype(jnp.bfloat16)
        raw = jnp.dot(grad_pre, tokens[...], preferred_element_type=jnp.float32)
        ratio = direction(first_ring[slot].astype(jnp.float32), second_ring[slot].astype(jnp.float32), raw, root)
        update_ring[slot] = ratio + decay_rate * weights

    def run(first_from, first_at, second_from, second_at):
        stream(
            second_count // tile,
            [
                (lambda step: first_from.at[rows(first_at, step)], first_ring, sems.at[0]),
                (lambda step: second_from.at[rows(second_at, step)], second_ring, sems.at[1]),
            ],
            [(lambda step: update_ring.at[lax.rem(step, DEPTH)], lambda step: update_out.at[rows(start, step)], sems.at[2])],
            compute,
        )

    second_count = got_second.shape[0]
    takes = flags[1] == 1

    @pl.when(takes)
    def _():
        run(got_first, start, got_second, 0)

    @pl.when(jnp.logical_not(takes))
    def _():
        run(first, start, second, start)


def adam_chunk(flags, held, parts, cot, first, second, got_first, got_second, start, base, before):
    rows, width = first.shape
    count = got_second.shape[0]
    tile = tile_of(count, ADAM_TILE)
    before = [] if before is None else [before]
    ring = lambda dtype: pltpu.VMEM((DEPTH, tile, width), dtype)
    return pl.pallas_call(
        functools.partial(adam_kernel, start, base, tile, math.sqrt(width), len(parts)),
        in_specs=[IN_SMEM, IN_VMEM, IN_VMEM] + [IN_HBM] * 4 + [IN_VMEM] * len(parts) + [IN_HBM] * len(before),
        out_specs=IN_HBM,
        out_shape=pltpu.HBM((rows, width), jnp.float32),
        input_output_aliases={7 + len(parts): 0} if before else {},
        scratch_shapes=[
            ring(jnp.bfloat16),
            ring(jnp.bfloat16),
            ring(jnp.float32),
            pltpu.VMEM((len(parts) * parts[0].shape[0], width), jnp.bfloat16),
            pltpu.SemaphoreType.DMA((3, DEPTH)),
        ],
        compiler_params=pltpu.CompilerParams(vmem_limit_bytes=ADAM_VMEM * 2**20),
        cost_estimate=pl.CostEstimate(flops=1000 * count * width, bytes_accessed=8 * count * width, transcendentals=2 * count * width),
        name="adam",
    )(flags, *in_vmem([held, cot]), *in_hbm([first, second, got_first]), got_second, *in_vmem(parts), *in_hbm(before))


def groups_of(shards):
    return max(size for size in range(1, shards + 1) if shards % size == 0 and size * size <= shards)


def gather_near(block, shards):
    group = groups_of(shards)
    pairs = lambda shift: [(i, i // group * group + (i % group + shift) % group) for i in range(shards)]
    return [block] + [lax.ppermute(block, "shard", pairs(shift)) for shift in range(1, group)]


def gather_far(block, shards):
    group = groups_of(shards)
    count = shards // group
    pairs = lambda shift: [(i, (i // group + shift) % count * group + i % group) for i in range(shards)]
    return [block] + [lax.ppermute(block, "shard", pairs(shift)) for shift in range(1, count)]


def sources(shards):
    group = groups_of(shards)
    count = shards // group
    me, slot = lax.axis_index("shard"), jnp.arange(shards, dtype=jnp.int32)
    return (me // group + count - slot // group) % count * group + (me % group + group - slot % group) % group


def pair_step(inner_params, anchor, momentum, first_moment, second_moment, activations, cotangent, spare_index, peer_index):
    position = lax.axis_index("replica")
    shards = lax.axis_size("shard")
    rows = anchor.shape[0]

    def swap(array):
        return lax.ppermute(array, "replica", [(0, 1), (1, 0)])

    spare, peer = spare_index[0], peer_index[0]
    flags = jnp.stack([position == spare, (position == spare) & (peer != position)]).astype(jnp.int32)
    inner, first, second = inner_params[0], first_moment[0], second_moment[0]

    here, cot = activations[0], cotangent[0]
    depth = here.shape[0]
    column = jnp.arange(shards * depth, dtype=jnp.int32)
    token_of = jnp.repeat(sources(shards), depth) * depth + column % depth
    token_of = jnp.pad(token_of, (0, -len(column) % LANES), constant_values=-1)
    inner, flags, token_of = lax.optimization_barrier((inner, flags, token_of))

    chunks = spans(rows, [sum(group) for group in PARTS])
    pieces = [
        (start + low, high, start, which)
        for which, ((start, count), group) in enumerate(zip(chunks, PARTS))
        for low, high in spans(count, group)
    ]
    own_inner, got_inner = [], []
    for chunk in chunks:
        if own_inner:
            inner, own_inner[-1] = lax.optimization_barrier((inner, own_inner[-1]))
        own_inner += fetch(inner, [chunk])
        got_inner.append(swap(own_inner[-1]))
    first, own_inner[-1] = lax.optimization_barrier((first, own_inner[-1]))
    got_first = swap(first)

    near = gather_near(here, shards)
    token = jnp.arange(cot.shape[1], dtype=jnp.int32)[:, None]
    place = (token == token_of[None, :]).astype(jnp.bfloat16)
    cot = jnp.dot(cot, place, preferred_element_type=jnp.float32).astype(jnp.bfloat16)

    state, helds, parts, got_second = None, [], None, []
    for (start, count), own, got in zip(chunks, own_inner, got_inner):
        *state, held = outer_chunk(flags, own, got, anchor, momentum, start, state)
        helds.append(held)
        if parts is None:
            near, second, state = lax.optimization_barrier((near, second, state))
            parts = gather_far(jnp.concatenate(near, 0), shards)
            for block in fetch(second, [piece[:2] for piece in pieces]):
                got_second.append(swap(block))
    parts, state = lax.optimization_barrier((parts, state))
    anchor_new, momentum_new = state

    update = None
    for (start, count, base, which), got in zip(pieces, got_second):
        update = adam_chunk(flags, helds[which], parts, cot, first, second, got_first, got, start, base, update)
    return anchor_new, momentum_new, update[None]


def from_root(block, axis, holder):
    block = jnp.where(lax.axis_index(axis) == holder, block, jnp.zeros_like(block))
    return lax.psum(block, axis)


def general_step(
    inner_params,
    anchor,
    momentum,
    first_moment,
    second_moment,
    activations,
    cotangent,
    spare_index,
    peer_index,
):
    replicas = lax.axis_size("replica")
    position = lax.axis_index("replica")
    spare_slot = spare_index[0]
    peer_slot = peer_index[0]
    healthy = (position != spare_slot).astype(jnp.float32)
    difference = (anchor - inner_params[0].astype(jnp.float32)) * healthy
    summed = lax.psum(difference, "replica")
    average = summed / (replicas - 1)
    momentum_new = nesterov_mu * momentum + average
    anchor_new = anchor - outer_rate * (average + nesterov_mu * momentum_new)
    received = (
        from_root(first_moment, "replica", peer_slot),
        from_root(second_moment, "replica", peer_slot),
    )
    is_spare = position == spare_slot
    first_used = jnp.where(is_spare, received[0], first_moment)[0].astype(jnp.float32)
    second_used = jnp.where(is_spare, received[1], second_moment)[0].astype(jnp.float32)
    weights = anchor_new.astype(jnp.bfloat16)
    root = math.sqrt(weights.shape[1])
    cot_local = cotangent[0]
    tokens_part = lax.all_gather(activations, "shard", axis=1, tiled=True)[0]
    pre = (
        lax.dot_general(
            weights, tokens_part, (((1,), (1,)), ((), ())), preferred_element_type=jnp.float32
        )
        / root
    )
    grad_pre = (cot_local.astype(jnp.float32) * slope(pre)).astype(jnp.bfloat16)
    gradient = jnp.dot(grad_pre, tokens_part, preferred_element_type=jnp.float32) / root
    first = beta_one * first_used + (1.0 - beta_one) * gradient
    second = beta_two * second_used + (1.0 - beta_two) * gradient * gradient
    update = first / bias_one / (jnp.sqrt(second / bias_two) + adam_eps) + decay_rate * anchor_new
    return (anchor_new, momentum_new, update[None])


def solution(mesh):
    placed = (
        P("replica", "shard", None),
        P("shard", None),
        P("shard", None),
        P("replica", "shard", None),
        P("replica", "shard", None),
        P("replica", "shard", None),
        P("replica", "shard", None),
        P("shard"),
        P("shard"),
    )
    local = pair_step if mesh.shape["replica"] == 2 else general_step
    return jax.shard_map(
        local,
        mesh=mesh,
        in_specs=placed,
        out_specs=(P("shard", None), P("shard", None), P("replica", "shard", None)),
        check_vma=False,
    )
```

```python
import functools
import math

import jax
import jax.numpy as jnp
from jax import lax
from jax.experimental import pallas as pl
from jax.experimental.pallas import tpu as pltpu
from jax.sharding import PartitionSpec as P


outer_rate = 0.7
nesterov_mu = 0.9
beta_one = 0.9
beta_two = 0.95
bias_one = 1.0 - 0.9**40
bias_two = 1.0 - 0.95**40
adam_eps = 1e-08
decay_rate = 0.1

UNIT = 16
OUTER_PARTS = (5, 10)
MOMENT_PARTS = ((5,), (10,))
OUTER_TILE = 16
ADAM_TILE = 64
BEND_TILE = 128
OUTER_DEPTH = 10
ADAM_DEPTH = 5
OUTER_VMEM = 12
ADAM_VMEM = 14


IN_VMEM = pl.BlockSpec(memory_space=pltpu.VMEM)
IN_HBM = pl.BlockSpec(memory_space=pl.ANY)
IN_SMEM = pl.BlockSpec(memory_space=pltpu.SMEM)


def in_hbm(arrays):
    return [pltpu.with_memory_space_constraint(array, pltpu.HBM) for array in arrays]


def in_vmem(arrays):
    return [pltpu.with_memory_space_constraint(array, pltpu.VMEM) for array in arrays]


def slope(pre):
    sigma = jax.nn.sigmoid(pre)
    return sigma * (1.0 + pre * (1.0 - sigma))


def spans(rows, parts):
    units, total, run, bounds = rows // UNIT, sum(parts), 0, [0]
    for part in parts:
        run += part
        bounds.append(units * run // total * UNIT)
    bounds[-1] = rows
    return [(low, high - low) for low, high in zip(bounds, bounds[1:]) if high > low]


def tile_of(count, limit):
    return max(tile for tile in range(UNIT, max(limit, UNIT) + 1, UNIT) if count % tile == 0)


def stream(depth, steps, loads, stores, compute, after=lambda step: None):
    def load(step):
        for source, ring, sems in loads:
            slot = lax.rem(step, ring.shape[0])
            pltpu.make_async_copy(source(step), ring.at[slot], sems.at[slot]).start()

    def wait_load(step):
        for source, ring, sems in loads:
            slot = lax.rem(step, ring.shape[0])
            pltpu.make_async_copy(source(step), ring.at[slot], sems.at[slot]).wait()

    def wait_store(step):
        for source, target, sems in stores:
            pltpu.make_async_copy(source(step), target(step), sems.at[lax.rem(step, depth)]).wait()

    for step in range(min(depth - 1, steps)):
        load(step)

    def body(step, carry):
        @pl.when(step + depth - 1 < steps)
        def _():
            load(step + depth - 1)

        wait_load(step)

        @pl.when(step >= depth)
        def _():
            wait_store(step - depth)

        compute(step, lax.rem(step, depth))
        for source, target, sems in stores:
            pltpu.make_async_copy(source(step), target(step), sems.at[lax.rem(step, depth)]).start()
        after(step)
        return carry

    lax.fori_loop(0, steps, body, 0)
    for step in range(max(0, steps - depth), steps):
        wait_store(step)


def fetch_kernel(starts, source, *rest):
    targets, sems = rest[:-1], rest[-1]
    copies = [
        pltpu.make_async_copy(source.at[pl.ds(start, target.shape[0])], target, sems.at[at])
        for at, (start, target) in enumerate(zip(starts, targets))
    ]
    for copy in copies:
        copy.start()
    for copy in copies:
        copy.wait()


def fetch(array, chunks):
    width = array.shape[1]
    return pl.pallas_call(
        functools.partial(fetch_kernel, [start for start, _ in chunks]),
        in_specs=[IN_HBM],
        out_specs=[IN_VMEM] * len(chunks),
        out_shape=[pltpu.VMEM((count, width), array.dtype) for _, count in chunks],
        scratch_shapes=[pltpu.SemaphoreType.DMA((len(chunks),))],
        compiler_params=pltpu.CompilerParams(vmem_limit_bytes=OUTER_VMEM * 2**20),
        cost_estimate=pl.CostEstimate(flops=0, bytes_accessed=4 * sum(count for _, count in chunks) * width, transcendentals=0),
        name="fetch",
    )(*in_hbm([array]))


def roles(spare_ref, peer_ref):
    position = lax.axis_index("replica")
    spare = spare_ref[0] == position
    return spare, spare & (peer_ref[0] != position)


def first_outer_kernel(start, spare_ref, peer_ref, own, got, anchor, momentum, cot, anchor_out, momentum_out, held, turned, *rings):
    def extra(step):
        @pl.when(step == 0)
        def _():
            turned[...] = cot[...].astype(jnp.float32).T.astype(turned.dtype)

    outer_stream(start, roles(spare_ref, peer_ref)[0], own, got, anchor, momentum, anchor_out, momentum_out, held, rings, extra, lambda step: None)


def last_outer_kernel(start, befores, pieces, shards, spare_ref, peer_ref, own, got, anchor, momentum, cot, *rest):
    parts, rest = rest[:pieces], rest[pieces:]
    earlier = rest[:befores]
    anchor_out, momentum_out, held, tokens, grad_pre = rest[befores + 2 : befores + 7]
    rings = rest[befores + 7 :]
    tile = rings[0].shape[1]
    root = math.sqrt(held.shape[1])

    steps = held.shape[0] // tile

    def bend(weights, at):
        pre = lax.dot_general(weights.astype(jnp.bfloat16), tokens[...], (((1,), (1,)), ((), ())), preferred_element_type=jnp.float32) * (1.0 / root)
        here = pl.ds(at, weights.shape[0])
        grad_pre[here, :] = (cot[here, :].astype(jnp.float32) * slope(pre)).astype(jnp.bfloat16)

    def extra(step):
        @pl.when(step == 0)
        def _():
            height = parts[0].shape[0]
            for index, part in enumerate(parts):
                tokens[index * height : (index + 1) * height, :] = part[...]
            count = tokens.shape[0]
            shape = (count, count)
            slot, token = lax.broadcasted_iota(jnp.int32, shape, 1), lax.broadcasted_iota(jnp.int32, shape, 0)
            origin = jnp.zeros(shape, jnp.int32)
            for block, source in enumerate(sources(shards)):
                first_slot = block * (count // shards)
                inside = (slot >= first_slot) & (slot < first_slot + count // shards)
                origin = jnp.where(inside, source * (count // shards) + slot - first_slot, origin)
            place = (token == origin).astype(jnp.float32).astype(tokens.dtype)
            tokens[...] = jnp.dot(place, tokens[...], preferred_element_type=jnp.float32).astype(tokens.dtype)

        for index, (before, low, size, at) in enumerate(blocks):

            @pl.when(step == index * steps // len(blocks))
            def _(before=before, low=low, size=size, at=at):
                bend(before[low : low + size, :], at)

    blocks, at = [], 0
    for before in earlier:
        size = tile_of(before.shape[0], BEND_TILE)
        blocks += [(before, low, size, at + low) for low in range(0, before.shape[0], size)]
        at += before.shape[0]
    size = max(tile, tile_of(held.shape[0], BEND_TILE) // tile * tile)

    def after(step):
        for low in range(0, held.shape[0], size):
            high = min(low + size, held.shape[0])

            @pl.when(step == high // tile - 1)
            def _(low=low, high=high):
                bend(held[low:high, :], start + low)

    outer_stream(start, roles(spare_ref, peer_ref)[0], own, got, anchor, momentum, anchor_out, momentum_out, held, rings, extra, after)


def outer_stream(start, spare, own, got, anchor, momentum, anchor_out, momentum_out, held, rings, extra, after):
    anchor_ring, momentum_ring, moved_ring, sems = rings
    tile = anchor_ring.shape[1]
    rows = lambda step: pl.ds(pl.multiple_of(start + step * tile, UNIT), tile)
    here = lambda step: pl.ds(pl.multiple_of(step * tile, UNIT), tile)

    def compute(step, slot):
        extra(step)

        def with_inner(inner):
            base = anchor_ring[slot]
            average = base - inner[rows(step), :].astype(jnp.float32)
            moved = nesterov_mu * momentum_ring[slot] + average
            moved_ring[slot] = moved
            held[here(step), :] = base - outer_rate * (average + nesterov_mu * moved)

        @pl.when(spare)
        def _():
            with_inner(got)

        @pl.when(jnp.logical_not(spare))
        def _():
            with_inner(own)

    stream(
        OUTER_DEPTH,
        held.shape[0] // tile,
        [
            (lambda step: anchor.at[rows(step)], anchor_ring, sems.at[0]),
            (lambda step: momentum.at[rows(step)], momentum_ring, sems.at[1]),
        ],
        [
            (lambda step: held.at[here(step)], lambda step: anchor_out.at[rows(step)], sems.at[2]),
            (lambda step: moved_ring.at[lax.rem(step, OUTER_DEPTH)], lambda step: momentum_out.at[rows(step)], sems.at[3]),
        ],
        compute,
        after,
    )


def outer_call(kernel, who, count, own, got, anchor, momentum, more, before, extra_shapes, extra_scratch):
    width = own.shape[1]
    tile = tile_of(count, OUTER_TILE)
    whole = pltpu.HBM(anchor.shape, jnp.float32)
    ring = pltpu.VMEM((OUTER_DEPTH, tile, width), jnp.float32)
    arrays, specs = [array for array, _ in more], [spec for _, spec in more]
    at = 6 + len(more)
    return pl.pallas_call(
        kernel,
        in_specs=[IN_SMEM, IN_SMEM, IN_VMEM, IN_VMEM, IN_HBM, IN_HBM] + specs + [IN_HBM] * len(before),
        out_specs=[IN_HBM, IN_HBM, IN_VMEM] + [IN_VMEM] * len(extra_shapes),
        out_shape=[whole, whole, pltpu.VMEM((count, width), jnp.float32)] + extra_shapes,
        input_output_aliases={at: 0, at + 1: 1} if before else {},
        scratch_shapes=[ring, ring, ring, pltpu.SemaphoreType.DMA((4, OUTER_DEPTH))] + extra_scratch,
        compiler_params=pltpu.CompilerParams(vmem_limit_bytes=OUTER_VMEM * 2**20),
        cost_estimate=pl.CostEstimate(flops=10 * count * width, bytes_accessed=16 * count * width, transcendentals=0),
        name="outer",
    )(*who, *in_vmem([own, got]), *in_hbm([anchor, momentum]), *arrays, *in_hbm(before))


def direction(first, second, raw, root):
    scale = math.sqrt((1.0 - beta_two) / bias_two) / root
    mean = first * (beta_one / bias_one / scale) + raw * ((1.0 - beta_one) / bias_one / root / scale)
    square = second * (beta_two / bias_two / scale**2) + raw * raw
    return mean * pltpu.reciprocal(square * lax.rsqrt(square) + adam_eps / scale, approx=False)


def adam_kernel(start, base, tile, spare_ref, peer_ref, held, grad_pre, tokens, first, second, got_first, got_second, *rest):
    update_out, first_ring, second_ring, update_ring, sems = rest[-5:]
    rows = lambda at, step: pl.ds(pl.multiple_of(at + step * tile, UNIT), tile)
    takes = roles(spare_ref, peer_ref)[1]

    def compute(step, slot):
        raw = jnp.dot(grad_pre[rows(start, step), :], tokens[...], preferred_element_type=jnp.float32)
        ratio = direction(first_ring[slot].astype(jnp.float32), second_ring[slot].astype(jnp.float32), raw, math.sqrt(held.shape[1]))
        update_ring[slot] = ratio + decay_rate * held[rows(start - base, step), :]

    def run(first_from, first_at, second_from, second_at):
        stream(
            ADAM_DEPTH,
            got_second.shape[0] // tile,
            [
                (lambda step: first_from.at[rows(first_at, step)], first_ring, sems.at[0]),
                (lambda step: second_from.at[rows(second_at, step)], second_ring, sems.at[1]),
            ],
            [(lambda step: update_ring.at[lax.rem(step, ADAM_DEPTH)], lambda step: update_out.at[rows(start, step)], sems.at[2])],
            compute,
        )

    @pl.when(takes)
    def _():
        run(got_first, start, got_second, 0)

    @pl.when(jnp.logical_not(takes))
    def _():
        run(first, start, second, start)


def adam_chunk(who, held, grad_pre, tokens, first, second, got_first, got_second, start, base, before):
    rows, width = first.shape
    count = got_second.shape[0]
    tile = tile_of(count, ADAM_TILE)
    before = [] if before is None else [before]
    ring = lambda dtype: pltpu.VMEM((ADAM_DEPTH, tile, width), dtype)
    return pl.pallas_call(
        functools.partial(adam_kernel, start, base, tile),
        in_specs=[IN_SMEM] * 2 + [IN_VMEM] * 3 + [IN_HBM] * (4 + len(before)),
        out_specs=IN_HBM,
        out_shape=pltpu.HBM((rows, width), jnp.float32),
        input_output_aliases={9: 0} if before else {},
        scratch_shapes=[ring(jnp.bfloat16), ring(jnp.bfloat16), ring(jnp.float32), pltpu.SemaphoreType.DMA((3, ADAM_DEPTH))],
        compiler_params=pltpu.CompilerParams(vmem_limit_bytes=ADAM_VMEM * 2**20),
        cost_estimate=pl.CostEstimate(flops=1000 * count * width, bytes_accessed=8 * count * width, transcendentals=2 * count * width),
        name="adam",
    )(*who, *in_vmem([held, grad_pre, tokens]), *in_hbm([first, second, got_first]), got_second, *in_hbm(before))


def groups_of(shards):
    return max(size for size in range(1, shards + 1) if shards % size == 0 and size * size <= shards)


def labelled(block, pairs):
    return lax.ppermute(block, "shard", pairs)


def gather_near(block, shards):
    group = groups_of(shards)
    pairs = lambda shift: [(i, i // group * group + (i % group + shift) % group) for i in range(shards)]
    return [block] + [labelled(block, pairs(shift)) for shift in range(1, group)]


def gather_far(block, shards):
    group = groups_of(shards)
    count = shards // group
    pairs = lambda shift: [(i, (i // group + shift) % count * group + i % group) for i in range(shards)]
    return [block] + [labelled(block, pairs(shift)) for shift in range(1, count)]


def sources(shards):
    group = groups_of(shards)
    count = shards // group
    me = lax.axis_index("shard")
    far, near = lax.div(me, group), lax.rem(me, group)
    return [
        lax.rem(far + count - shift_far, count) * group + lax.rem(near + group - shift_near, group)
        for shift_far in range(count)
        for shift_near in range(group)
    ]


def pair_step(inner_params, anchor, momentum, first_moment, second_moment, activations, cotangent, spare_index, peer_index):
    shards = lax.axis_size("shard")
    rows, width = anchor.shape

    def swap(array):
        return lax.ppermute(array, "replica", [(0, 1), (1, 0)])

    who = (spare_index, peer_index)
    inner, first, second = inner_params[0], first_moment[0], second_moment[0]
    here, cot = activations[0], cotangent[0]
    chunks = spans(rows, OUTER_PARTS)
    portions = [
        (start + low, high, start, which)
        for which, ((start, count), group) in enumerate(zip(chunks, MOMENT_PARTS))
        for low, high in spans(count, group)
    ]
    got_inner = swap(inner)
    got_first = swap(first)
    near = gather_near(here, shards)
    blocks = fetch(second, [portion[:2] for portion in portions])
    got_second = [swap(block) for block in blocks]
    parts = gather_far(jnp.concatenate(near, 0), shards)

    def outer(piece, kernel, *more):
        start, count = piece
        return outer_call(functools.partial(kernel, start), who, count, inner, got_inner, anchor, momentum, *more)

    *state, held, turned = outer(chunks[0], first_outer_kernel, [(in_vmem([cot.T])[0], IN_VMEM)], [], [pltpu.VMEM(cot.shape, cot.dtype)], [])
    helds = [held]
    anchor_new, momentum_new, held, tokens, grad_pre = outer(
        chunks[1],
        lambda start, *refs: last_outer_kernel(start, len(helds), len(parts), shards, *refs),
        [(array, IN_VMEM) for array in in_vmem([turned, *parts, *helds])],
        state,
        [pltpu.VMEM((shards * here.shape[0], width), here.dtype), pltpu.VMEM(cot.shape, cot.dtype)],
        [],
    )
    helds.append(held)
    update = None
    for (start, count, base, which), got in zip(portions, got_second):
        update = adam_chunk(who, helds[which], grad_pre, tokens, first, second, got_first, got, start, base, update)
    return anchor_new, momentum_new, update[None]


def from_root(block, axis, holder):
    block = jnp.where(lax.axis_index(axis) == holder, block, jnp.zeros_like(block))
    return lax.psum(block, axis)


def general_step(
    inner_params,
    anchor,
    momentum,
    first_moment,
    second_moment,
    activations,
    cotangent,
    spare_index,
    peer_index,
):
    replicas = lax.axis_size("replica")
    position = lax.axis_index("replica")
    spare_slot = spare_index[0]
    peer_slot = peer_index[0]
    healthy = (position != spare_slot).astype(jnp.float32)
    difference = (anchor - inner_params[0].astype(jnp.float32)) * healthy
    summed = lax.psum(difference, "replica")
    average = summed / (replicas - 1)
    momentum_new = nesterov_mu * momentum + average
    anchor_new = anchor - outer_rate * (average + nesterov_mu * momentum_new)
    received = (
        from_root(first_moment, "replica", peer_slot),
        from_root(second_moment, "replica", peer_slot),
    )
    is_spare = position == spare_slot
    first_used = jnp.where(is_spare, received[0], first_moment)[0].astype(jnp.float32)
    second_used = jnp.where(is_spare, received[1], second_moment)[0].astype(jnp.float32)
    weights = anchor_new.astype(jnp.bfloat16)
    root = math.sqrt(weights.shape[1])
    cot_local = cotangent[0]
    tokens_part = lax.all_gather(activations, "shard", axis=1, tiled=True)[0]
    pre = (
        lax.dot_general(
            weights, tokens_part, (((1,), (1,)), ((), ())), preferred_element_type=jnp.float32
        )
        / root
    )
    grad_pre = (cot_local.astype(jnp.float32) * slope(pre)).astype(jnp.bfloat16)
    gradient = jnp.dot(grad_pre, tokens_part, preferred_element_type=jnp.float32) / root
    first = beta_one * first_used + (1.0 - beta_one) * gradient
    second = beta_two * second_used + (1.0 - beta_two) * gradient * gradient
    update = first / bias_one / (jnp.sqrt(second / bias_two) + adam_eps) + decay_rate * anchor_new
    return (anchor_new, momentum_new, update[None])


def solution(mesh):
    placed = (
        P("replica", "shard", None),
        P("shard", None),
        P("shard", None),
        P("replica", "shard", None),
        P("replica", "shard", None),
        P("replica", "shard", None),
        P("replica", "shard", None),
        P("shard"),
        P("shard"),
    )
    local = pair_step if mesh.shape["replica"] == 2 else general_step
    return jax.shard_map(
        local,
        mesh=mesh,
        in_specs=placed,
        out_specs=(P("shard", None), P("shard", None), P("replica", "shard", None)),
        check_vma=False,
    )
```
